32 devices in a mesh: dp: 2 (over core), row: 4 (over y, x), col: 4 (over z).
Axes of the slice: x: 2, y: 2, z: 4, core: 2. Of those that a mesh axis runs over, the one named last changes fastest.
Arguments:
- block_input: float32 [1024, 1024], P(('dp', 'col'), 'row'), may hold values from -36 to 36
- out_cot: float32 [1024, 1024], P(('dp', 'col'), 'row'), may hold values from -6 to 6
- proj_weight: float32 [1024, 3, 1024], P('row', None, ('dp', 'col')), may hold values from -0.1875 to 0.1875
- conv_weight: float32 [3, 1024], P(None, ('dp', 'col')), may hold values from -3.5 to 3.5
- mixer_weight: float32 [1024, 1024], P(('dp', 'col'), 'row'), may hold values from -0.1875 to 0.1875
- up_weight: float32 [1024, 2, 4608], P('row', None, ('dp', 'col')), may hold values from -0.1875 to 0.1875
- down_weight: float32 [4608, 1024], P(('dp', 'col'), 'row'), may hold values from -0.09375 to 0.09375
- norm_gains: float32 [2, 1024], P(None, 'row'), may hold values from 0.25 to 1.75
- proj_moments: float32 [2, 1024, 3, 1024], P(None, 'row', None, ('dp', 'col')), may hold values from -1024 to 1024, as said below
- conv_moments: float32 [2, 3, 1024], P(None, None, ('dp', 'col')), may hold values from -1024 to 1024, as said below
- mixer_moments: float32 [2, 1024, 1024], P(None, ('dp', 'col'), 'row'), may hold values from -1024 to 1024, as said below
- up_moments: float32 [2, 1024, 2, 4608], P(None, 'row', None, ('dp', 'col')), may hold values from -1024 to 1024, as said below
- down_moments: float32 [2, 4608, 1024], P(None, ('dp', 'col'), 'row'), may hold values from -1024 to 1024, as said below
- gains_moments: float32 [2, 2, 1024], P(None, None, 'row'), may hold values from -1024 to 1024, as said below
Outputs:
- block_output: float32 [1024, 1024], P(('dp', 'col'), 'row')
- input_grad: float32 [1024, 1024], P(('dp', 'col'), 'row')
- proj_grad: float32 [1024, 3, 1024], P('row', None, ('dp', 'col'))
- conv_grad: float32 [3, 1024], P(None, ('dp', 'col'))
- mixer_grad: float32 [1024, 1024], P(('dp', 'col'), 'row')
- up_grad: float32 [1024, 2, 4608], P('row', None, ('dp', 'col'))
- down_grad: float32 [4608, 1024], P(('dp', 'col'), 'row')
- gains_grad: float32 [2, 1024], P(None, 'row')
- proj_new: float32 [1024, 3, 1024], P('row', None, ('dp', 'col'))
- conv_new: float32 [3, 1024], P(None, ('dp', 'col'))
- mixer_new: float32 [1024, 1024], P(('dp', 'col'), 'row')
- up_new: float32 [1024, 2, 4608], P('row', None, ('dp', 'col'))
- down_new: float32 [4608, 1024], P(('dp', 'col'), 'row')
- gains_new: float32 [2, 1024], P(None, 'row')
- proj_moments_new: float32 [2, 1024, 3, 1024], P(None, 'row', None, ('dp', 'col'))
- conv_moments_new: float32 [2, 3, 1024], P(None, None, ('dp', 'col'))
- mixer_moments_new: float32 [2, 1024, 1024], P(None, ('dp', 'col'), 'row')
- up_moments_new: float32 [2, 1024, 2, 4608], P(None, 'row', None, ('dp', 'col'))
- down_moments_new: float32 [2, 4608, 1024], P(None, ('dp', 'col'), 'row')
- gains_moments_new: float32 [2, 2, 1024], P(None, None, 'row')
The draws below stay inside these ranges and needn't reach their ends.
Inputs may be any that keep to these rules, and one draw needn't show every extreme that they name: `proj_moments`: index 0 of the leading dimension holds first moments, index 1 second moments, which are positive. `conv_moments`: index 0 of the leading dimension holds first moments, index 1 second moments, which are positive. `mixer_moments`: index 0 of the leading dimension holds first moments, index 1 second moments, which are positive. `up_moments`: index 0 of the leading dimension holds first moments, index 1 second moments, which are positive. `down_moments`: index 0 of the leading dimension holds first moments, index 1 second moments, which are positive. `gains_moments`: index 0 of the leading dimension holds first moments, index 1 second moments, which are positive.
All inputs are finite; a program needn't handle non-finite values.
Results may differ from the reference program's by a relative error of at most 0.012.
The reference program's roundings to bfloat16 on the way count: a program that leaves them out, or rounds other values in their place, can miss the bound.
Values may be sent and summed in bfloat16 or wider, within the bound.
A program may use at most 128 MiB of HBM per device.

```python
import math
import jax
import jax.numpy as jnp
from jax import lax

D = 1024
FF = 4608
KERNEL = 3
STEP = 4
LEN = 512
TOKENS = 1024
N_DP = 2


def draw_block_input(key, part):
    noise_key, scale_key = jax.random.split(jax.random.fold_in(key, 3))
    columns = jnp.exp(math.log(0.3) + math.log(10.0) * jnp.arange(D, dtype=jnp.float32) / (D - 1))
    noise_field = jnp.clip(jax.random.normal(noise_key, (TOKENS, D), jnp.float32), -4.0, 4.0)
    row_scale = jnp.exp(jax.random.uniform(scale_key, (TOKENS, 1), jnp.float32, math.log(0.4), math.log(2.5)))
    return noise_field * row_scale * columns[None, :]


def moment_pair(key, shape):
    first_key, second_key = jax.random.split(jax.random.fold_in(key, 11))
    spread = 0.2 * jnp.sqrt(jnp.float32(TOKENS))
    first_moment = jnp.clip(jax.random.normal(first_key, shape, jnp.float32), -3.0, 3.0) * spread
    second_moment = jnp.exp(jax.random.uniform(second_key, shape, jnp.float32, math.log(0.0004), math.log(0.004))) * jnp.float32(TOKENS)
    return jnp.stack([first_moment, second_moment])


def draw_proj_moments(key, part):
    return moment_pair(key, (D, 3, D))


def draw_conv_moments(key, part):
    return moment_pair(key, (KERNEL, D))


def draw_mixer_moments(key, part):
    return moment_pair(key, (D, D))


def draw_up_moments(key, part):
    return moment_pair(key, (D, 2, FF))


def draw_down_moments(key, part):
    return moment_pair(key, (FF, D))


def draw_gains_moments(key, part):
    return moment_pair(key, (2, D))


def block_scale(key, shape, shards, smallest, top_value):
    def one(position, blocks):
        steps = jax.random.uniform(jax.random.fold_in(jax.random.fold_in(key, 6), position), (blocks,), jnp.float32, smallest / len(shards), top_value / len(shards))
        return jnp.repeat(jnp.exp(steps), shape[position] // blocks).reshape((-1,) + (1,) * (len(shape) - position - 1))

    gain = one(*shards[0])
    for cut in shards[1:]:
        gain = gain * one(*cut)
    return gain


def normal_values(stream_key, shape, scale, most, cuts=(), kind=jnp.bfloat16):
    entries = scale * jax.random.normal(stream_key, shape, jnp.float32)
    if cuts:
        entries = entries * block_scale(stream_key, shape, cuts, -0.22, 0.18)
    return jnp.clip(entries, -most, most).astype(kind)


def setup_inputs(seed: int = 0) -> dict:
    arg_keys = jax.random.split(jax.random.key(seed), 15)
    return {
        "block_input": draw_block_input(jax.random.fold_in(arg_keys[14], 71), 0),
        "out_cot": normal_values(arg_keys[1], (TOKENS, D), 1.0, 6.0, ((0, 8), (1, 4)), jnp.float32),
        "proj_weight": normal_values(arg_keys[2], (D, 3, D), D ** -0.5, 0.1875, ((0, 4), (2, 8)), jnp.float32),
        "conv_weight": normal_values(arg_keys[3], (KERNEL, D), KERNEL ** -0.5, 3.5, ((1, 8),), jnp.float32),
        "mixer_weight": normal_values(arg_keys[4], (D, D), D ** -0.5, 0.1875, ((0, 8), (1, 4)), jnp.float32),
        "up_weight": normal_values(arg_keys[5], (D, 2, FF), D ** -0.5, 0.1875, ((0, 4), (2, 8)), jnp.float32),
        "down_weight": normal_values(arg_keys[6], (FF, D), FF ** -0.5, 0.09375, ((0, 8), (1, 4)), jnp.float32),
        "norm_gains": jnp.clip(1.0 + 0.15 * jax.random.normal(arg_keys[7], (2, D), jnp.float32), 0.25, 1.75),
        "proj_moments": draw_proj_moments(jax.random.fold_in(arg_keys[14], 71), 0),
        "conv_moments": draw_conv_moments(jax.random.fold_in(arg_keys[14], 71), 0),
        "mixer_moments": draw_mixer_moments(jax.random.fold_in(arg_keys[14], 71), 0),
        "up_moments": draw_up_moments(jax.random.fold_in(arg_keys[14], 71), 0),
        "down_moments": draw_down_moments(jax.random.fold_in(arg_keys[14], 71), 0),
        "gains_moments": draw_gains_moments(jax.random.fold_in(arg_keys[14], 71), 0),
    }


eps_norm = 1e-05
beta_first = 0.9
beta_second = 0.999
eps_adam = 1e-08
matrix_rate = 0.01
small_rate = 0.1
decay_rate = 0.1

def plain_product(left_side, right_side):
    return jnp.dot(left_side, right_side, preferred_element_type=jnp.float32)

def contract_rows(left_side, right_side):
    return lax.dot_general(left_side, right_side, (((0,), (0,)), ((), ())), preferred_element_type=jnp.float32)

def contract_cols(left_side, right_side):
    return lax.dot_general(left_side, right_side, (((1,), (1,)), ((), ())), preferred_element_type=jnp.float32)

def adam_step(parameter, gradient, moments, step_rate, decay_weight):
    first_moment = beta_first * moments[0] + (1.0 - beta_first) * gradient
    second_moment = beta_second * moments[1] + (1.0 - beta_second) * gradient * gradient
    first_hat = first_moment / (1.0 - beta_first ** STEP)
    second_hat = second_moment / (1.0 - beta_second ** STEP)
    update = first_hat / (jnp.sqrt(second_hat) + eps_adam) + decay_weight * parameter
    return (parameter - step_rate * update, jnp.stack([first_moment, second_moment]))

def reference(block_input, out_cot, proj_weight, conv_weight, mixer_weight, up_weight, down_weight, norm_gains, proj_moments, conv_moments, mixer_moments, up_moments, down_moments, gains_moments):
    proj_low = proj_weight.astype(jnp.bfloat16).reshape(D, 3 * D)
    conv_taps = lax.optimization_barrier(conv_weight.astype(jnp.bfloat16)).astype(jnp.float32)
    mixer_low = mixer_weight.astype(jnp.bfloat16)
    up_low = up_weight.astype(jnp.bfloat16).reshape(D, 2 * FF)
    down_low = down_weight.astype(jnp.bfloat16)
    gain_one = norm_gains[0]
    gain_two = norm_gains[1]
    history = KERNEL - 1
    padding = jnp.zeros((history, D), jnp.float32)

    def one_sequence(totals, inputs):
        residual, cotangent = inputs
        inverse_one = lax.rsqrt(lax.optimization_barrier(jnp.mean(residual * residual, axis=1, keepdims=True)) + eps_norm)
        normed_one = (residual * inverse_one * gain_one).astype(jnp.bfloat16)
        projected = plain_product(normed_one, proj_low)
        gate_b = projected[:, :D]
        gate_c = projected[:, D:2 * D]
        values_x = projected[:, 2 * D:]
        mixed_input = gate_b * values_x
        padded = jnp.concatenate([padding, mixed_input], axis=0)
        convolved = conv_taps[0] * padded[0:LEN]
        for offset in range(1, KERNEL):
            convolved = convolved + conv_taps[offset] * padded[offset:offset + LEN]
        gated = (gate_c * convolved).astype(jnp.bfloat16)
        residual_two = residual + plain_product(gated, mixer_low)
        inverse_two = lax.rsqrt(lax.optimization_barrier(jnp.mean(residual_two * residual_two, axis=1, keepdims=True)) + eps_norm)
        normed_two = (residual_two * inverse_two * gain_two).astype(jnp.bfloat16)
        gate_up = plain_product(normed_two, up_low)
        gate_pre = gate_up[:, :FF]
        lifted = gate_up[:, FF:]
        sigmoid_gate = jax.nn.sigmoid(gate_pre)
        swish_gate = gate_pre * sigmoid_gate
        hidden = (swish_gate * lifted).astype(jnp.bfloat16)
        output = residual_two + plain_product(hidden, down_low)
        cot_low = cotangent.astype(jnp.bfloat16)
        d_hidden = contract_cols(cot_low, down_low)
        d_gate = d_hidden * lifted * sigmoid_gate * (1.0 + gate_pre * (1.0 - sigmoid_gate))
        d_lifted = d_hidden * swish_gate
        d_gate_up = jnp.concatenate([d_gate, d_lifted], axis=1).astype(jnp.bfloat16)
        down_part = contract_rows(hidden, cot_low)
        up_part = contract_rows(normed_two, d_gate_up)
        d_normed_two = contract_cols(d_gate_up, up_low)
        scaled_two = d_normed_two * gain_two
        gain_two_part = lax.optimization_barrier(jnp.sum(d_normed_two * residual_two * inverse_two, axis=0))
        d_residual = cotangent + inverse_two * (scaled_two - residual_two * inverse_two * inverse_two * lax.optimization_barrier(jnp.mean(scaled_two * residual_two, axis=1, keepdims=True)))
        d_residual_low = d_residual.astype(jnp.bfloat16)
        d_gated = contract_cols(d_residual_low, mixer_low)
        mixer_part = contract_rows(gated, d_residual_low)
        d_convolved = d_gated * gate_c
        d_gate_c = d_gated * convolved
        extended = jnp.concatenate([d_convolved, padding], axis=0)
        d_mixed = conv_taps[history] * extended[0:LEN]
        for offset in range(1, KERNEL):
            d_mixed = d_mixed + conv_taps[history - offset] * extended[offset:offset + LEN]
        conv_part = jnp.stack([lax.optimization_barrier(jnp.sum(d_convolved * padded[offset:offset + LEN], axis=0)) for offset in range(KERNEL)])
        d_projected = jnp.concatenate([d_mixed * values_x, d_gate_c, d_mixed * gate_b], axis=1).astype(jnp.bfloat16)
        proj_part = contract_rows(normed_one, d_projected)
        d_normed_one = contract_cols(d_projected, proj_low)
        scaled_one = d_normed_one * gain_one
        gain_one_part = lax.optimization_barrier(jnp.sum(d_normed_one * residual * inverse_one, axis=0))
        d_input = d_residual + inverse_one * (scaled_one - residual * inverse_one * inverse_one * lax.optimization_barrier(jnp.mean(scaled_one * residual, axis=1, keepdims=True)))
        parts = (proj_part, conv_part, mixer_part, up_part, down_part, jnp.stack([gain_one_part, gain_two_part]))
        new_totals = tuple((total_value + part_value for total_value, part_value in zip(totals, parts)))
        return (new_totals, (output, d_input))
    zeros_init = (jnp.zeros((D, 3 * D), jnp.float32), jnp.zeros((KERNEL, D), jnp.float32), jnp.zeros((D, D), jnp.float32), jnp.zeros((D, 2 * FF), jnp.float32), jnp.zeros((FF, D), jnp.float32), jnp.zeros((2, D), jnp.float32))
    sequences = (block_input.reshape(N_DP, LEN, D), out_cot.reshape(N_DP, LEN, D))
    totals, (outputs, input_grads) = lax.scan(one_sequence, zeros_init, sequences)
    proj_grad = totals[0].reshape(D, 3, D)
    conv_grad = totals[1]
    mixer_grad = totals[2]
    up_grad = totals[3].reshape(D, 2, FF)
    down_grad = totals[4]
    gains_grad = totals[5]
    proj_new, proj_moments_new = adam_step(proj_weight, proj_grad, proj_moments, matrix_rate, decay_rate)
    conv_new, conv_moments_new = adam_step(conv_weight, conv_grad, conv_moments, small_rate, 0.0)
    mixer_new, mixer_moments_new = adam_step(mixer_weight, mixer_grad, mixer_moments, matrix_rate, decay_rate)
    up_new, up_moments_new = adam_step(up_weight, up_grad, up_moments, matrix_rate, decay_rate)
    down_new, down_moments_new = adam_step(down_weight, down_grad, down_moments, matrix_rate, decay_rate)
    gains_new, gains_moments_new = adam_step(norm_gains, gains_grad, gains_moments, small_rate, 0.0)
    return (outputs.reshape(TOKENS, D), input_grads.reshape(TOKENS, D), proj_grad, conv_grad, mixer_grad, up_grad, down_grad, gains_grad, proj_new, conv_new, mixer_new, up_new, down_new, gains_new, proj_moments_new, conv_moments_new, mixer_moments_new, up_moments_new, down_moments_new, gains_moments_new)
```

```python
import itertools
import math

import jax
import jax.numpy as jnp
from jax import lax
from jax.experimental import pallas as pl
from jax.experimental.pallas import tpu as pltpu
from jax.sharding import PartitionSpec as P

D = 1024
KERNEL = 3
STEP = 4


eps_norm = 1e-05
beta_first = 0.9
beta_second = 0.999
eps_adam = 1e-08
matrix_rate = 0.01
small_rate = 0.1
decay_rate = 0.1


def shifted(x, axis, by):
    devices = lax.axis_size(axis)
    pairs = [(i, i + by) for i in range(devices) if 0 <= i + by < devices]
    return lax.ppermute(x, axis, pairs)


def plain_product(left_side, right_side):
    return jnp.dot(left_side, right_side, preferred_element_type=jnp.float32)


def contract_rows(left_side, right_side):
    return lax.dot_general(
        left_side, right_side, (((0,), (0,)), ((), ())), preferred_element_type=jnp.float32
    )


def contract_cols(left_side, right_side):
    return lax.dot_general(
        left_side, right_side, (((1,), (1,)), ((), ())), preferred_element_type=jnp.float32
    )


def adam_step(parameter, gradient, moments, step_rate, decay_weight):
    first_moment = beta_first * moments[0] + (1.0 - beta_first) * gradient
    second_moment = beta_second * moments[1] + (1.0 - beta_second) * gradient * gradient
    first_hat = first_moment / (1.0 - beta_first**STEP)
    second_hat = second_moment / (1.0 - beta_second**STEP)
    update = first_hat / (jnp.sqrt(second_hat) + eps_adam) + decay_weight * parameter
    return (parameter - step_rate * update, jnp.stack([first_moment, second_moment]))


def exchange(ids, axes, gathers=(), swaps=()):
    sizes = [lax.axis_size(axis) for axis in axes]
    devices = math.prod(sizes)
    arrays = tuple(gathers) + tuple(swaps)
    count, whole = len(arrays), len(gathers)
    shapes = [x.shape for x in gathers] + [x.shape[1:] for x in swaps]

    def kernel(*refs):
        sources, targets = refs[:count], refs[count : 2 * count]
        send_sem, recv_sem, own_sem = refs[2 * count :]
        me = jnp.int32(0)
        for axis, size in zip(axes, sizes):
            me = me * size + lax.axis_index(axis)

        def coordinates(index):
            place = {}
            for axis, size in reversed(list(zip(axes, sizes))):
                place[axis] = lax.rem(index, size)
                index = index // size
            return place

        peers = [lax.rem(me + step, devices) for step in range(1, devices)]
        barrier = pltpu.get_barrier_semaphore()
        for peer in peers:
            pl.semaphore_signal(
                barrier,
                inc=1,
                device_id=coordinates(peer),
                device_id_type=pl.DeviceIdType.MESH,
            )
        pl.semaphore_wait(barrier, devices - 1)
        remote, own = [], []
        for item in range(count):
            for step, peer in enumerate(peers):
                copy = pltpu.make_async_remote_copy(
                    src_ref=sources[item] if item < whole else sources[item].at[peer],
                    dst_ref=targets[item].at[me],
                    send_sem=send_sem.at[item, step],
                    recv_sem=recv_sem.at[item, step],
                    device_id=coordinates(peer),
                    device_id_type=pl.DeviceIdType.MESH,
                )
                copy.start()
                remote.append(copy)
        for item in range(count):
            copy = pltpu.make_async_copy(
                sources[item] if item < whole else sources[item].at[me],
                targets[item].at[me],
                own_sem.at[item],
            )
            copy.start()
            own.append(copy)
        for copy in own + remote:
            copy.wait()

    return pl.pallas_call(
        kernel,
        out_shape=[
            jax.ShapeDtypeStruct((devices,) + tuple(shape), x.dtype)
            for shape, x in zip(shapes, arrays)
        ],
        in_specs=[pl.BlockSpec(memory_space=pl.ANY)] * count,
        out_specs=[pl.BlockSpec(memory_space=pltpu.VMEM)] * count,
        scratch_shapes=[
            pltpu.SemaphoreType.DMA((count, devices - 1)),
            pltpu.SemaphoreType.DMA((count, devices - 1)),
            pltpu.SemaphoreType.DMA((count,)),
        ],
        compiler_params=pltpu.CompilerParams(collective_id=next(ids), has_side_effects=True),
    )(*arrays)


def flat_rows(gathered):
    return gathered.reshape((-1,) + gathered.shape[2:])


def row_blocks(partial, axis):
    devices = lax.axis_size(axis)
    return partial.astype(jnp.bfloat16).reshape((devices, -1) + partial.shape[1:])


def added(blocks):
    total = blocks[0].astype(jnp.float32)
    for index in range(1, blocks.shape[0]):
        total = total + blocks[index].astype(jnp.float32)
    return total


def width_total(ids, row_values):
    (parts,) = exchange(ids, ("row",), gathers=[row_values[None, :]])
    return added(parts)[0]


def inverse_rms(ids, residual):
    row_total = width_total(ids, jnp.sum(residual * residual, axis=1))
    return lax.rsqrt(row_total / D + eps_norm)[:, None]


def norm_back(ids, residual, inverse, gain_row, d_normed):
    scaled = d_normed * gain_row
    row_total = width_total(ids, jnp.sum(scaled * residual, axis=1))[:, None] / D
    d_residual = inverse * (scaled - residual * inverse * inverse * row_total)
    gain_part = jnp.sum(d_normed * residual * inverse, axis=0)
    return (d_residual, gain_part)


def on_device(
    block_input,
    out_cot,
    proj_weight,
    conv_weight,
    mixer_weight,
    up_weight,
    down_weight,
    norm_gains,
    proj_moments,
    conv_moments,
    mixer_moments,
    up_moments,
    down_moments,
    gains_moments,
):
    ids = itertools.count()
    low = jnp.bfloat16
    wide_proj, conv_wide, wide_mixer, wide_up, wide_down = exchange(
        ids,
        ("dp",),
        gathers=[
            proj_weight.astype(low).transpose(1, 0, 2),
            conv_weight.astype(low),
            mixer_weight.astype(low),
            up_weight.astype(low).transpose(1, 0, 2),
            down_weight.astype(low),
        ],
    )
    replicas = wide_proj.shape[0]
    width_local = proj_weight.shape[0]
    shard_width = proj_weight.shape[2]
    shard_units = up_weight.shape[2]
    channels = replicas * shard_width
    units = replicas * shard_units
    proj_matrix = wide_proj.transpose(2, 1, 0, 3).reshape(width_local, 3 * channels)
    up_matrix = wide_up.transpose(2, 1, 0, 3).reshape(width_local, 2 * units)
    wide_mixer = flat_rows(wide_mixer)
    wide_down = flat_rows(wide_down)
    conv_taps = conv_wide.transpose(1, 0, 2).reshape(KERNEL, channels).astype(jnp.float32)
    gain_one = norm_gains[0]
    gain_two = norm_gains[1]
    history = KERNEL - 1
    inverse_one = inverse_rms(ids, block_input)
    normed_one = (block_input * inverse_one * gain_one).astype(low)
    gathered_one, gathered_cot = map(
        flat_rows, exchange(ids, ("col",), gathers=[normed_one, out_cot.astype(low)])
    )
    inner_rows = gathered_one.shape[0] // lax.axis_size("row")
    projected, d_hidden = map(
        added,
        exchange(
            ids,
            ("row",),
            swaps=[
                row_blocks(plain_product(gathered_one, proj_matrix), "row"),
                row_blocks(contract_cols(gathered_cot, wide_down), "row"),
            ],
        ),
    )
    gate_b = projected[:, :channels]
    gate_c = projected[:, channels : 2 * channels]
    values_x = projected[:, 2 * channels :]
    mixed_input = gate_b * values_x
    left_rim = shifted(mixed_input[inner_rows - history :], "row", 1)
    padded = jnp.concatenate([left_rim, mixed_input], axis=0)
    convolved = conv_taps[0] * padded[0:inner_rows]
    for offset in range(1, KERNEL):
        convolved = convolved + conv_taps[offset] * padded[offset : offset + inner_rows]
    gated = (gate_c * convolved).astype(low)
    gathered_gated = flat_rows(exchange(ids, ("row",), gathers=[gated])[0])
    mixer_out = added(
        exchange(
            ids,
            ("col",),
            swaps=[row_blocks(plain_product(gathered_gated, wide_mixer), "col")],
        )[0]
    )
    residual_two = block_input + mixer_out
    inverse_two = inverse_rms(ids, residual_two)
    normed_two = (residual_two * inverse_two * gain_two).astype(low)
    gathered_two = flat_rows(exchange(ids, ("col",), gathers=[normed_two])[0])
    gate_up = added(
        exchange(
            ids, ("row",), swaps=[row_blocks(plain_product(gathered_two, up_matrix), "row")]
        )[0]
    )
    gate_pre = gate_up[:, :units]
    lifted = gate_up[:, units:]
    sigmoid_gate = jax.nn.sigmoid(gate_pre)
    swish_gate = gate_pre * sigmoid_gate
    hidden = (swish_gate * lifted).astype(low)
    d_gate = d_hidden * lifted * sigmoid_gate * (1.0 + gate_pre * (1.0 - sigmoid_gate))
    d_lifted = d_hidden * swish_gate
    d_gate_up = jnp.concatenate([d_gate, d_lifted], axis=1).astype(low)
    gathered_hidden, gathered_dgate = map(
        flat_rows, exchange(ids, ("row",), gathers=[hidden, d_gate_up])
    )
    ffn_out, d_normed_two = map(
        added,
        exchange(
            ids,
            ("col",),
            swaps=[
                row_blocks(plain_product(gathered_hidden, wide_down), "col"),
                row_blocks(contract_cols(gathered_dgate, up_matrix), "col"),
            ],
        ),
    )
    block_output = residual_two + ffn_out
    down_part = contract_rows(gathered_hidden, gathered_cot)
    up_part = contract_rows(gathered_two, gathered_dgate)
    d_norm_two, gain_two_part = norm_back(ids, residual_two, inverse_two, gain_two, d_normed_two)
    d_residual = out_cot + d_norm_two
    gathered_dres = flat_rows(exchange(ids, ("col",), gathers=[d_residual.astype(low)])[0])
    d_gated = added(
        exchange(
            ids,
            ("row",),
            swaps=[row_blocks(contract_cols(gathered_dres, wide_mixer), "row")],
        )[0]
    )
    mixer_part = contract_rows(gathered_gated, gathered_dres)
    d_convolved = d_gated * gate_c
    d_gate_c = d_gated * convolved
    next_rim = shifted(d_convolved[:history], "row", -1)
    extended = jnp.concatenate([d_convolved, next_rim], axis=0)
    d_mixed = conv_taps[history] * extended[0:inner_rows]
    for offset in range(1, KERNEL):
        d_mixed = d_mixed + conv_taps[history - offset] * extended[offset : offset + inner_rows]
    conv_part = jnp.stack(
        [
            jnp.sum(d_convolved * padded[offset : offset + inner_rows], axis=0)
            for offset in range(KERNEL)
        ]
    )
    d_projected = jnp.concatenate([d_mixed * values_x, d_gate_c, d_mixed * gate_b], axis=1).astype(
        low
    )
    gathered_dproj = flat_rows(exchange(ids, ("row",), gathers=[d_projected])[0])
    proj_part = contract_rows(gathered_one, gathered_dproj)
    d_normed_one = added(
        exchange(
            ids,
            ("col",),
            swaps=[row_blocks(contract_cols(gathered_dproj, proj_matrix), "col")],
        )[0]
    )
    d_norm_one, gain_one_part = norm_back(ids, block_input, inverse_one, gain_one, d_normed_one)
    input_grad = d_residual + d_norm_one
    proj_grad, mixer_grad, up_grad, down_grad = map(
        added,
        exchange(
            ids,
            ("dp",),
            swaps=[
                proj_part.astype(low)
                .reshape(width_local, 3, replicas, shard_width)
                .transpose(2, 1, 0, 3),
                row_blocks(mixer_part, "dp"),
                up_part.astype(low)
                .reshape(width_local, 2, replicas, shard_units)
                .transpose(2, 1, 0, 3),
                row_blocks(down_part, "dp"),
            ],
        ),
    )
    proj_grad = proj_grad.transpose(1, 0, 2)
    up_grad = up_grad.transpose(1, 0, 2)
    conv_total = added(exchange(ids, ("dp", "row"), gathers=[conv_part])[0])
    conv_grad = lax.dynamic_slice_in_dim(
        conv_total, lax.axis_index("dp") * shard_width, shard_width, 1
    )
    gains_part = jnp.stack([gain_one_part, gain_two_part])
    gains_grad = added(exchange(ids, ("dp", "col"), gathers=[gains_part])[0])
    proj_new, proj_moments_new = adam_step(
        proj_weight, proj_grad, proj_moments, matrix_rate, decay_rate
    )
    conv_new, conv_moments_new = adam_step(conv_weight, conv_grad, conv_moments, small_rate, 0.0)
    mixer_new, mixer_moments_new = adam_step(
        mixer_weight, mixer_grad, mixer_moments, matrix_rate, decay_rate
    )
    up_new, up_moments_new = adam_step(up_weight, up_grad, up_moments, matrix_rate, decay_rate)
    down_new, down_moments_new = adam_step(
        down_weight, down_grad, down_moments, matrix_rate, decay_rate
    )
    gains_new, gains_moments_new = adam_step(norm_gains, gains_grad, gains_moments, small_rate, 0.0)
    return (
        block_output,
        input_grad,
        proj_grad,
        conv_grad,
        mixer_grad,
        up_grad,
        down_grad,
        gains_grad,
        proj_new,
        conv_new,
        mixer_new,
        up_new,
        down_new,
        gains_new,
        proj_moments_new,
        conv_moments_new,
        mixer_moments_new,
        up_moments_new,
        down_moments_new,
        gains_moments_new,
    )


def solution(mesh):
    in_specs = (
        P(("dp", "col"), "row"),
        P(("dp", "col"), "row"),
        P("row", None, ("dp", "col")),
        P(None, ("dp", "col")),
        P(("dp", "col"), "row"),
        P("row", None, ("dp", "col")),
        P(("dp", "col"), "row"),
        P(None, "row"),
        P(None, "row", None, ("dp", "col")),
        P(None, None, ("dp", "col")),
        P(None, ("dp", "col"), "row"),
        P(None, "row", None, ("dp", "col")),
        P(None, ("dp", "col"), "row"),
        P(None, None, "row"),
    )
    out_specs = (
        P(("dp", "col"), "row"),
        P(("dp", "col"), "row"),
        P("row", None, ("dp", "col")),
        P(None, ("dp", "col")),
        P(("dp", "col"), "row"),
        P("row", None, ("dp", "col")),
        P(("dp", "col"), "row"),
        P(None, "row"),
        P("row", None, ("dp", "col")),
        P(None, ("dp", "col")),
        P(("dp", "col"), "row"),
        P("row", None, ("dp", "col")),
        P(("dp", "col"), "row"),
        P(None, "row"),
        P(None, "row", None, ("dp", "col")),
        P(None, None, ("dp", "col")),
        P(None, ("dp", "col"), "row"),
        P(None, "row", None, ("dp", "col")),
        P(None, ("dp", "col"), "row"),
        P(None, None, "row"),
    )
    return jax.shard_map(
        on_device, mesh=mesh, in_specs=in_specs, out_specs=out_specs, check_vma=False
    )
```

```python
import itertools
import math

import jax
import jax.numpy as jnp
from jax import lax
from jax.experimental import pallas as pl
from jax.experimental.pallas import tpu as pltpu
from jax.sharding import PartitionSpec as P

D = 1024
KERNEL = 3
STEP = 4


eps_norm = 1e-05
beta_first = 0.9
beta_second = 0.999
eps_adam = 1e-08
matrix_rate = 0.01
small_rate = 0.1
decay_rate = 0.1


def shifted(x, axis, by):
    devices = lax.axis_size(axis)
    pairs = [(i, i + by) for i in range(devices) if 0 <= i + by < devices]
    return lax.ppermute(x, axis, pairs)


def plain_product(left_side, right_side):
    return jnp.dot(left_side, right_side, preferred_element_type=jnp.float32)


def contract_rows(left_side, right_side):
    return lax.dot_general(
        left_side, right_side, (((0,), (0,)), ((), ())), preferred_element_type=jnp.float32
    )


def contract_cols(left_side, right_side):
    return lax.dot_general(
        left_side, right_side, (((1,), (1,)), ((), ())), preferred_element_type=jnp.float32
    )


def adam_step(parameter, gradient, moments, step_rate, decay_weight):
    first_moment = beta_first * moments[0] + (1.0 - beta_first) * gradient
    second_moment = beta_second * moments[1] + (1.0 - beta_second) * gradient * gradient
    first_hat = first_moment / (1.0 - beta_first**STEP)
    second_hat = second_moment / (1.0 - beta_second**STEP)
    update = first_hat / (jnp.sqrt(second_hat) + eps_adam) + decay_weight * parameter
    is_first = lax.broadcasted_iota(jnp.int32, moments.shape, 0) == 0
    moments_new = jnp.where(
        is_first,
        beta_first * moments + (1.0 - beta_first) * gradient[None],
        beta_second * moments + (1.0 - beta_second) * gradient[None] * gradient[None],
    )
    return (parameter - step_rate * update, moments_new)


def exchange(ids, *items):
    count = len(items)
    groups = []
    for axes, _, _ in items:
        if axes not in groups:
            groups.append(axes)
    sizes = {axes: [lax.axis_size(axis) for axis in axes] for axes in groups}
    devices = {axes: math.prod(sizes[axes]) for axes in groups}
    most = max(devices.values())

    def kernel(*refs):
        sources, targets = refs[:count], refs[count : 2 * count]
        send_sem, recv_sem, own_sem = refs[2 * count :]
        mine, peers = {}, {}
        for axes in groups:
            me = jnp.int32(0)
            for axis, size in zip(axes, sizes[axes]):
                me = me * size + lax.axis_index(axis)
            mine[axes] = me
            peers[axes] = []
            for step in range(1, devices[axes]):
                peer = lax.rem(me + step, devices[axes])
                place, index = {}, peer
                for axis, size in reversed(list(zip(axes, sizes[axes]))):
                    place[axis] = lax.rem(index, size)
                    index = index // size
                peers[axes].append((peer, place))
        barrier = pltpu.get_barrier_semaphore()
        for axes in groups:
            for _, place in peers[axes]:
                pl.semaphore_signal(
                    barrier, inc=1, device_id=place, device_id_type=pl.DeviceIdType.MESH
                )
        pl.semaphore_wait(barrier, sum(len(peers[axes]) for axes in groups))
        copies = []
        for item, (axes, _, whole) in enumerate(items):
            for step, (peer, place) in enumerate(peers[axes]):
                copies.append(
                    pltpu.make_async_remote_copy(
                        src_ref=sources[item] if whole else sources[item].at[peer],
                        dst_ref=targets[item].at[mine[axes]],
                        send_sem=send_sem.at[item, step],
                        recv_sem=recv_sem.at[item, step],
                        device_id=place,
                        device_id_type=pl.DeviceIdType.MESH,
                    )
                )
        for item, (axes, _, whole) in enumerate(items):
            copies.append(
                pltpu.make_async_copy(
                    sources[item] if whole else sources[item].at[mine[axes]],
                    targets[item].at[mine[axes]],
                    own_sem.at[item],
                )
            )
        for copy in copies:
            copy.start()
        for copy in copies:
            copy.wait()

    return pl.pallas_call(
        kernel,
        out_shape=[
            jax.ShapeDtypeStruct(
                (devices[axes],) + tuple(x.shape if whole else x.shape[1:]), x.dtype
            )
            for axes, x, whole in items
        ],
        in_specs=[pl.BlockSpec(memory_space=pl.ANY)] * count,
        out_specs=[pl.BlockSpec(memory_space=pltpu.VMEM)] * count,
        scratch_shapes=[
            pltpu.SemaphoreType.DMA((count, most - 1)),
            pltpu.SemaphoreType.DMA((count, most - 1)),
            pltpu.SemaphoreType.DMA((count,)),
        ],
        compiler_params=pltpu.CompilerParams(collective_id=next(ids), has_side_effects=True),
    )(*[x for _, x, _ in items])


DP, ROW, COL = ("dp",), ("row",), ("col",)


def gather(axes, x):
    return (axes, x, True)


def swap(axes, x):
    blocks = math.prod(lax.axis_size(axis) for axis in axes)
    low = x.astype(jnp.bfloat16)
    return (axes, low.reshape((blocks, -1) + x.shape[1:]), False)


def flat_rows(gathered):
    return gathered.reshape((-1,) + gathered.shape[2:])


def added(blocks):
    total = blocks[0].astype(jnp.float32)
    for index in range(1, blocks.shape[0]):
        total = total + blocks[index].astype(jnp.float32)
    return total


def inverse_rms(row_total):
    return lax.rsqrt(row_total / D + eps_norm)[:, None]


def square_sums(residual):
    return jnp.sum(residual * residual, axis=1)[None, :]


def back_sums(residual, gain_row, d_normed):
    return jnp.sum(d_normed * gain_row * residual, axis=1)[None, :]


def norm_back(residual, inverse, gain_row, d_normed, row_total):
    scaled = d_normed * gain_row
    row_mean = row_total[:, None] / D
    return inverse * (scaled - residual * inverse * inverse * row_mean)


def gain_sums(residual, inverse, d_normed):
    return jnp.sum(d_normed * residual * inverse, axis=0)


def on_device(
    block_input,
    out_cot,
    proj_weight,
    conv_weight,
    mixer_weight,
    up_weight,
    down_weight,
    norm_gains,
    proj_moments,
    conv_moments,
    mixer_moments,
    up_moments,
    down_moments,
    gains_moments,
):
    ids = itertools.count()
    low = jnp.bfloat16
    up_turned = up_weight.transpose(1, 2, 0)
    up_low = up_turned.astype(low)
    stats, wide_proj, conv_wide, wide_mixer, wide_gate, wide_lift, wide_down = exchange(
        ids,
        gather(ROW, square_sums(block_input)),
        gather(DP, proj_weight.astype(low).transpose(1, 0, 2)),
        gather(DP, conv_weight.astype(low)),
        gather(DP, mixer_weight.astype(low)),
        gather(DP, up_low[0]),
        gather(DP, up_low[1]),
        gather(DP, down_weight.astype(low)),
    )
    replicas = wide_proj.shape[0]
    width_local = proj_weight.shape[0]
    shard_width = proj_weight.shape[2]
    channels = replicas * shard_width
    proj_matrix = wide_proj.transpose(2, 1, 0, 3).reshape(width_local, 3 * channels)
    wide_mixer, wide_gate, wide_lift, wide_down = map(
        flat_rows, (wide_mixer, wide_gate, wide_lift, wide_down)
    )
    conv_taps = conv_wide.transpose(1, 0, 2).reshape(KERNEL, channels).astype(jnp.float32)
    gain_one = norm_gains[0]
    gain_two = norm_gains[1]
    history = KERNEL - 1
    inverse_one = inverse_rms(added(stats)[0])
    normed_one = (block_input * inverse_one * gain_one).astype(low)
    gathered_one = flat_rows(exchange(ids, gather(COL, normed_one))[0])
    projected, gathered_cot = exchange(
        ids,
        swap(ROW, plain_product(gathered_one, proj_matrix)),
        gather(COL, out_cot.astype(low)),
    )
    projected = added(projected)
    gathered_cot = flat_rows(gathered_cot)
    inner_rows = projected.shape[0]
    half = wide_down.shape[0] // 256 * 128 or wide_down.shape[0] // 2
    gate_b = projected[:, :channels]
    gate_c = projected[:, channels : 2 * channels]
    values_x = projected[:, 2 * channels :]
    mixed_input = gate_b * values_x
    left_rim = shifted(mixed_input[inner_rows - history :], "row", 1)
    padded = jnp.concatenate([left_rim, mixed_input], axis=0)
    convolved = conv_taps[0] * padded[0:inner_rows]
    for offset in range(1, KERNEL):
        convolved = convolved + conv_taps[offset] * padded[offset : offset + inner_rows]
    gated = (gate_c * convolved).astype(low)
    gathered_gated = flat_rows(exchange(ids, gather(ROW, gated))[0])
    mixer_out, d_hidden_a = exchange(
        ids,
        swap(COL, plain_product(gathered_gated, wide_mixer)),
        swap(ROW, contract_cols(gathered_cot, wide_down[:half])),
    )
    residual_two = block_input + added(mixer_out)
    (stats,) = exchange(ids, gather(ROW, square_sums(residual_two)))
    inverse_two = inverse_rms(added(stats)[0])
    normed_two = (residual_two * inverse_two * gain_two).astype(low)
    gathered_two, d_hidden_b = exchange(
        ids,
        gather(COL, normed_two),
        swap(ROW, contract_cols(gathered_cot, wide_down[half:])),
    )
    gathered_two = flat_rows(gathered_two)
    d_hidden = jnp.concatenate([added(d_hidden_a), added(d_hidden_b)], axis=1)
    gate_pre, lifted = map(
        added,
        exchange(
            ids,
            swap(ROW, contract_cols(gathered_two, wide_gate)),
            swap(ROW, contract_cols(gathered_two, wide_lift)),
        ),
    )
    sigmoid_gate = jax.nn.sigmoid(gate_pre)
    swish_gate = gate_pre * sigmoid_gate
    hidden = (swish_gate * lifted).astype(low)
    d_gate = d_hidden * lifted * sigmoid_gate * (1.0 + gate_pre * (1.0 - sigmoid_gate))
    d_lifted = d_hidden * swish_gate
    gathered_dgate, gathered_dlift = map(
        flat_rows,
        exchange(ids, gather(ROW, d_gate.astype(low)), gather(ROW, d_lifted.astype(low))),
    )
    hidden_half = inner_rows // 2
    d_normed_two, hidden_a = exchange(
        ids,
        swap(
            COL,
            plain_product(gathered_dgate, wide_gate) + plain_product(gathered_dlift, wide_lift),
        ),
        gather(ROW, hidden[:hidden_half]),
    )
    d_normed_two = added(d_normed_two)
    (stats,) = exchange(ids, gather(ROW, back_sums(residual_two, gain_two, d_normed_two)))
    d_residual = out_cot + norm_back(
        residual_two, inverse_two, gain_two, d_normed_two, added(stats)[0]
    )
    gathered_dres, hidden_b = exchange(
        ids, gather(COL, d_residual.astype(low)), gather(ROW, hidden[hidden_half:])
    )
    gathered_dres = flat_rows(gathered_dres)
    gathered_hidden = flat_rows(jnp.concatenate([hidden_a, hidden_b], axis=1))
    (d_gated,) = exchange(ids, swap(ROW, contract_cols(gathered_dres, wide_mixer)))
    d_gated = added(d_gated)
    d_convolved = d_gated * gate_c
    d_gate_c = d_gated * convolved
    next_rim = shifted(d_convolved[:history], "row", -1)
    extended = jnp.concatenate([d_convolved, next_rim], axis=0)
    d_mixed = conv_taps[history] * extended[0:inner_rows]
    for offset in range(1, KERNEL):
        d_mixed = d_mixed + conv_taps[history - offset] * extended[offset : offset + inner_rows]
    conv_part = jnp.stack(
        [
            jnp.sum(d_convolved * padded[offset : offset + inner_rows], axis=0)
            for offset in range(KERNEL)
        ]
    )
    d_projected = jnp.concatenate([d_mixed * values_x, d_gate_c, d_mixed * gate_b], axis=1).astype(
        low
    )
    gathered_dproj, ffn_out, conv_parts = exchange(
        ids,
        gather(ROW, d_projected),
        swap(COL, plain_product(gathered_hidden, wide_down)),
        gather(("dp", "row"), conv_part),
    )
    gathered_dproj = flat_rows(gathered_dproj)
    block_output = residual_two + added(ffn_out)
    proj_part = contract_rows(gathered_one, gathered_dproj).astype(low)
    proj_part = proj_part.reshape(width_local, 3, replicas, shard_width).transpose(2, 1, 0, 3)
    d_normed_one, proj_grad, mixer_grad, up_grad_gate, up_grad_lift, down_grad = map(
        added,
        exchange(
            ids,
            swap(COL, contract_cols(gathered_dproj, proj_matrix)),
            (DP, proj_part, False),
            swap(DP, contract_rows(gathered_gated, gathered_dres)),
            swap(DP, contract_rows(gathered_dgate, gathered_two)),
            swap(DP, contract_rows(gathered_dlift, gathered_two)),
            swap(DP, contract_rows(gathered_hidden, gathered_cot)),
        ),
    )
    gains_part = jnp.stack(
        [
            gain_sums(block_input, inverse_one, d_normed_one),
            gain_sums(residual_two, inverse_two, d_normed_two),
        ]
    )
    stats, gains_parts = exchange(
        ids,
        gather(ROW, back_sums(block_input, gain_one, d_normed_one)),
        gather(("dp", "col"), gains_part),
    )
    input_grad = d_residual + norm_back(
        block_input, inverse_one, gain_one, d_normed_one, added(stats)[0]
    )
    proj_grad = proj_grad.transpose(1, 0, 2)
    up_grad = jnp.stack([up_grad_gate, up_grad_lift]).transpose(2, 0, 1)
    conv_grad = lax.dynamic_slice_in_dim(
        added(conv_parts), lax.axis_index("dp") * shard_width, shard_width, 1
    )
    gains_grad = added(gains_parts)
    proj_new, proj_moments_new = adam_step(
        proj_weight, proj_grad, proj_moments, matrix_rate, decay_rate
    )
    conv_new, conv_moments_new = adam_step(conv_weight, conv_grad, conv_moments, small_rate, 0.0)
    mixer_new, mixer_moments_new = adam_step(
        mixer_weight, mixer_grad, mixer_moments, matrix_rate, decay_rate
    )
    up_new, up_moments_new = adam_step(up_weight, up_grad, up_moments, matrix_rate, decay_rate)
    down_new, down_moments_new = adam_step(
        down_weight, down_grad, down_moments, matrix_rate, decay_rate
    )
    gains_new, gains_moments_new = adam_step(norm_gains, gains_grad, gains_moments, small_rate, 0.0)
    return (
        block_output,
        input_grad,
        proj_grad,
        conv_grad,
        mixer_grad,
        up_grad,
        down_grad,
        gains_grad,
        proj_new,
        conv_new,
        mixer_new,
        up_new,
        down_new,
        gains_new,
        proj_moments_new,
        conv_moments_new,
        mixer_moments_new,
        up_moments_new,
        down_moments_new,
        gains_moments_new,
    )


def solution(mesh):
    in_specs = (
        P(("dp", "col"), "row"),
        P(("dp", "col"), "row"),
        P("row", None, ("dp", "col")),
        P(None, ("dp", "col")),
        P(("dp", "col"), "row"),
        P("row", None, ("dp", "col")),
        P(("dp", "col"), "row"),
        P(None, "row"),
        P(None, "row", None, ("dp", "col")),
        P(None, None, ("dp", "col")),
        P(None, ("dp", "col"), "row"),
        P(None, "row", None, ("dp", "col")),
        P(None, ("dp", "col"), "row"),
        P(None, None, "row"),
    )
    out_specs = (
        P(("dp", "col"), "row"),
        P(("dp", "col"), "row"),
        P("row", None, ("dp", "col")),
        P(None, ("dp", "col")),
        P(("dp", "col"), "row"),
        P("row", None, ("dp", "col")),
        P(("dp", "col"), "row"),
        P(None, "row"),
        P("row", None, ("dp", "col")),
        P(None, ("dp", "col")),
        P(("dp", "col"), "row"),
        P("row", None, ("dp", "col")),
        P(("dp", "col"), "row"),
        P(None, "row"),
        P(None, "row", None, ("dp", "col")),
        P(None, None, ("dp", "col")),
        P(None, ("dp", "col"), "row"),
        P(None, "row", None, ("dp", "col")),
        P(None, ("dp", "col"), "row"),
        P(None, None, "row"),
    )
    return jax.shard_map(
        on_device, mesh=mesh, in_specs=in_specs, out_specs=out_specs, check_vma=False
    )
```

```python
import itertools
import math

import jax
import jax.numpy as jnp
from jax import lax
from jax.experimental import pallas as pl
from jax.experimental.pallas import tpu as pltpu
from jax.sharding import PartitionSpec as P

D = 1024
KERNEL = 3
STEP = 4


eps_norm = 1e-05
beta_first = 0.9
beta_second = 0.999
eps_adam = 1e-08
matrix_rate = 0.01
small_rate = 0.1
decay_rate = 0.1


def plain_product(left_side, right_side):
    return jnp.dot(left_side, right_side, preferred_element_type=jnp.float32)


def contract_rows(left_side, right_side):
    return lax.dot_general(
        left_side, right_side, (((0,), (0,)), ((), ())), preferred_element_type=jnp.float32
    )


def contract_cols(left_side, right_side):
    return lax.dot_general(
        left_side, right_side, (((1,), (1,)), ((), ())), preferred_element_type=jnp.float32
    )


def adam_step(parameter, gradient, moments, step_rate, decay_weight):
    first_moment = beta_first * moments[0] + (1.0 - beta_first) * gradient
    second_moment = beta_second * moments[1] + (1.0 - beta_second) * gradient * gradient
    first_hat = first_moment / (1.0 - beta_first**STEP)
    second_hat = second_moment / (1.0 - beta_second**STEP)
    update = first_hat / (jnp.sqrt(second_hat) + eps_adam) + decay_weight * parameter
    is_first = lax.broadcasted_iota(jnp.int32, moments.shape, 0) == 0
    moments_new = jnp.where(
        is_first,
        beta_first * moments + (1.0 - beta_first) * gradient[None],
        beta_second * moments + (1.0 - beta_second) * gradient[None] * gradient[None],
    )
    return (parameter - step_rate * update, moments_new)


def exchange(ids, *items):
    count = len(items)
    groups = []
    for axes, _, _ in items:
        if axes not in groups:
            groups.append(axes)
    sizes = {axes: [lax.axis_size(axis) for axis in axes] for axes in groups}
    devices = {axes: math.prod(sizes[axes]) for axes in groups}
    most = max(devices.values())

    def kernel(*refs):
        sources, targets = refs[:count], refs[count : 2 * count]
        send_sem, recv_sem, own_sem = refs[2 * count :]
        mine, peers = {}, {}
        for axes in groups:
            me = jnp.int32(0)
            for axis, size in zip(axes, sizes[axes]):
                me = me * size + lax.axis_index(axis)
            mine[axes] = me
            peers[axes] = []
            for step in range(1, devices[axes]):
                peer = lax.rem(me + step, devices[axes])
                place, index = {}, peer
                for axis, size in reversed(list(zip(axes, sizes[axes]))):
                    place[axis] = lax.rem(index, size)
                    index = index // size
                peers[axes].append((peer, place))
        barrier = pltpu.get_barrier_semaphore()
        for axes in groups:
            for _, place in peers[axes]:
                pl.semaphore_signal(
                    barrier, inc=1, device_id=place, device_id_type=pl.DeviceIdType.MESH
                )
        pl.semaphore_wait(barrier, sum(len(peers[axes]) for axes in groups))
        copies = []
        for item, (axes, _, whole) in enumerate(items):
            for step, (peer, place) in enumerate(peers[axes]):
                copies.append(
                    pltpu.make_async_remote_copy(
                        src_ref=sources[item] if whole else sources[item].at[peer],
                        dst_ref=targets[item].at[mine[axes]],
                        send_sem=send_sem.at[item, step],
                        recv_sem=recv_sem.at[item, step],
                        device_id=place,
                        device_id_type=pl.DeviceIdType.MESH,
                    )
                )
        for item, (axes, _, whole) in enumerate(items):
            copies.append(
                pltpu.make_async_copy(
                    sources[item] if whole else sources[item].at[mine[axes]],
                    targets[item].at[mine[axes]],
                    own_sem.at[item],
                )
            )
        for copy in copies:
            copy.start()
        for copy in copies:
            copy.wait()

    return pl.pallas_call(
        kernel,
        out_shape=[
            jax.ShapeDtypeStruct(
                (devices[axes],) + tuple(x.shape if whole else x.shape[1:]), x.dtype
            )
            for axes, x, whole in items
        ],
        in_specs=[pl.BlockSpec(memory_space=pl.ANY)] * count,
        out_specs=[pl.BlockSpec(memory_space=pltpu.VMEM)] * count,
        scratch_shapes=[
            pltpu.SemaphoreType.DMA((count, most - 1)),
            pltpu.SemaphoreType.DMA((count, most - 1)),
            pltpu.SemaphoreType.DMA((count,)),
        ],
        compiler_params=pltpu.CompilerParams(collective_id=next(ids), has_side_effects=True),
    )(*[x for _, x, _ in items])


DP, ROW, COL = ("dp",), ("row",), ("col",)


def gather(axes, x):
    return (axes, x, True)


def swap(axes, x):
    blocks = math.prod(lax.axis_size(axis) for axis in axes)
    low = x.astype(jnp.bfloat16)
    return (axes, low.reshape((blocks, -1) + x.shape[1:]), False)


def flat_rows(gathered):
    return gathered.reshape((-1,) + gathered.shape[2:])


def added(blocks):
    total = blocks[0].astype(jnp.float32)
    for index in range(1, blocks.shape[0]):
        total = total + blocks[index].astype(jnp.float32)
    return total


def inverse_rms(row_total):
    return lax.rsqrt(row_total / D + eps_norm)[:, None]


def square_sums(residual):
    return jnp.sum(residual * residual, axis=1)[None, :]


def back_sums(residual, gain_row, d_normed):
    return jnp.sum(d_normed * gain_row * residual, axis=1)[None, :]


def norm_back(residual, inverse, gain_row, d_normed, row_total):
    scaled = d_normed * gain_row
    row_mean = row_total[:, None] / D
    return inverse * (scaled - residual * inverse * inverse * row_mean)


def gain_sums(residual, inverse, d_normed):
    return jnp.sum(d_normed * residual * inverse, axis=0)


def on_device(
    block_input,
    out_cot,
    proj_weight,
    conv_weight,
    mixer_weight,
    up_weight,
    down_weight,
    norm_gains,
    proj_moments,
    conv_moments,
    mixer_moments,
    up_moments,
    down_moments,
    gains_moments,
):
    ids = itertools.count()
    low = jnp.bfloat16
    up_turned = up_weight.transpose(1, 2, 0)
    up_low = up_turned.astype(low)
    stats, wide_proj, conv_wide, wide_mixer, wide_gate, wide_lift, wide_down = exchange(
        ids,
        gather(ROW, square_sums(block_input)),
        gather(DP, proj_weight.astype(low).transpose(1, 0, 2)),
        gather(DP, conv_weight.astype(low)),
        gather(DP, mixer_weight.astype(low)),
        gather(DP, up_low[0]),
        gather(DP, up_low[1]),
        gather(DP, down_weight.astype(low)),
    )
    replicas = wide_proj.shape[0]
    width_local = proj_weight.shape[0]
    shard_width = proj_weight.shape[2]
    channels = replicas * shard_width
    proj_matrix = wide_proj.transpose(2, 1, 0, 3).reshape(width_local, 3 * channels)
    wide_mixer, wide_gate, wide_lift, wide_down = map(
        flat_rows, (wide_mixer, wide_gate, wide_lift, wide_down)
    )
    conv_taps = conv_wide.transpose(1, 0, 2).reshape(KERNEL, channels).astype(jnp.float32)
    gain_one = norm_gains[0]
    gain_two = norm_gains[1]
    history = KERNEL - 1
    inverse_one = inverse_rms(added(stats)[0])
    normed_one = (block_input * inverse_one * gain_one).astype(low)
    gathered_one = flat_rows(exchange(ids, gather(COL, normed_one))[0])
    projected_item = swap(ROW, plain_product(gathered_one, proj_matrix))
    before_blocks = jnp.roll(projected_item[1][:, -history:], 1, axis=0)
    projected, before, gathered_cot = exchange(
        ids,
        projected_item,
        (ROW, before_blocks, False),
        gather(COL, out_cot.astype(low)),
    )
    before = added(before)
    projected = added(projected)
    gathered_cot = flat_rows(gathered_cot)
    inner_rows = projected.shape[0]
    half = wide_down.shape[0] // 256 * 128 or wide_down.shape[0] // 2
    gate_b = projected[:, :channels]
    gate_c = projected[:, channels : 2 * channels]
    values_x = projected[:, 2 * channels :]
    mixed_input = gate_b * values_x
    row_index = lax.axis_index("row")
    before_mixed = before[:, :channels] * before[:, 2 * channels :]
    left_rim = jnp.where(row_index > 0, before_mixed, 0.0)
    padded = jnp.concatenate([left_rim, mixed_input], axis=0)
    convolved = conv_taps[0] * padded[0:inner_rows]
    for offset in range(1, KERNEL):
        convolved = convolved + conv_taps[offset] * padded[offset : offset + inner_rows]
    gated = (gate_c * convolved).astype(low)
    gathered_gated, gate_rims = exchange(ids, gather(ROW, gated), gather(ROW, gate_c[:history]))
    gathered_gated = flat_rows(gathered_gated)
    row_devices = lax.axis_size("row")
    gate_after = lax.dynamic_index_in_dim(
        gate_rims, lax.rem(row_index + 1, row_devices), 0, keepdims=False
    )
    mixer_out, d_hidden_a = exchange(
        ids,
        swap(COL, plain_product(gathered_gated, wide_mixer)),
        swap(ROW, contract_cols(gathered_cot, wide_down[:half])),
    )
    residual_two = block_input + added(mixer_out)
    (stats,) = exchange(ids, gather(ROW, square_sums(residual_two)))
    inverse_two = inverse_rms(added(stats)[0])
    normed_two = (residual_two * inverse_two * gain_two).astype(low)
    gathered_two, d_hidden_b = exchange(
        ids,
        gather(COL, normed_two),
        swap(ROW, contract_cols(gathered_cot, wide_down[half:])),
    )
    gathered_two = flat_rows(gathered_two)
    d_hidden = jnp.concatenate([added(d_hidden_a), added(d_hidden_b)], axis=1)
    gate_pre, lifted = map(
        added,
        exchange(
            ids,
            swap(ROW, contract_cols(gathered_two, wide_gate)),
            swap(ROW, contract_cols(gathered_two, wide_lift)),
        ),
    )
    sigmoid_gate = jax.nn.sigmoid(gate_pre)
    swish_gate = gate_pre * sigmoid_gate
    hidden = (swish_gate * lifted).astype(low)
    d_gate = d_hidden * lifted * sigmoid_gate * (1.0 + gate_pre * (1.0 - sigmoid_gate))
    d_lifted = d_hidden * swish_gate
    d_gate = d_gate.astype(low)
    d_lifted = d_lifted.astype(low)
    unit_sums = jnp.sum(d_gate * gate_pre + d_lifted * lifted, axis=1)[None, :]
    gathered_dgate, gathered_dlift, unit_sums = exchange(
        ids, gather(ROW, d_gate), gather(ROW, d_lifted), gather(ROW, unit_sums)
    )
    gathered_dgate, gathered_dlift = map(flat_rows, (gathered_dgate, gathered_dlift))
    token_sums = unit_sums.reshape(lax.axis_size("col"), 1, -1)
    d_normed_two, hidden_a, token_sums = exchange(
        ids,
        swap(
            COL,
            plain_product(gathered_dgate, wide_gate) + plain_product(gathered_dlift, wide_lift),
        ),
        gather(ROW, hidden[:, :half]),
        (COL, token_sums, False),
    )
    d_normed_two = added(d_normed_two)
    d_residual = out_cot + norm_back(
        residual_two, inverse_two, gain_two, d_normed_two, added(token_sums)[0] / inverse_two[:, 0]
    )
    gathered_dres, hidden_b = exchange(
        ids, gather(COL, d_residual.astype(low)), gather(ROW, hidden[:, half:])
    )
    gathered_dres = flat_rows(gathered_dres)
    hidden_a, hidden_b = map(flat_rows, (hidden_a, hidden_b))
    d_gated_item = swap(ROW, contract_cols(gathered_dres, wide_mixer))
    after_blocks = jnp.roll(d_gated_item[1][:, :history], -1, axis=0)
    d_gated, d_gated_after = map(
        added, exchange(ids, d_gated_item, (ROW, after_blocks, False))
    )
    d_convolved = d_gated * gate_c
    d_gate_c = d_gated * convolved
    next_rim = jnp.where(row_index < row_devices - 1, d_gated_after * gate_after, 0.0)
    extended = jnp.concatenate([d_convolved, next_rim], axis=0)
    d_mixed = conv_taps[history] * extended[0:inner_rows]
    for offset in range(1, KERNEL):
        d_mixed = d_mixed + conv_taps[history - offset] * extended[offset : offset + inner_rows]
    conv_part = jnp.stack(
        [
            jnp.sum(d_convolved * padded[offset : offset + inner_rows], axis=0)
            for offset in range(KERNEL)
        ]
    )
    d_projected = jnp.concatenate([d_mixed * values_x, d_gate_c, d_mixed * gate_b], axis=1).astype(
        low
    )
    gathered_dproj, ffn_out, conv_parts = exchange(
        ids,
        gather(ROW, d_projected),
        swap(
            COL,
            plain_product(hidden_a, wide_down[:half]) + plain_product(hidden_b, wide_down[half:]),
        ),
        gather(("dp", "row"), conv_part),
    )
    gathered_dproj = flat_rows(gathered_dproj)
    block_output = residual_two + added(ffn_out)
    down_part = jnp.concatenate(
        [
            contract_rows(hidden_a, gathered_cot).astype(low),
            contract_rows(hidden_b, gathered_cot).astype(low),
        ],
        axis=0,
    )
    proj_part = contract_rows(gathered_one, gathered_dproj).astype(low)
    proj_part = proj_part.reshape(width_local, 3, replicas, shard_width).transpose(2, 1, 0, 3)
    d_normed_one, proj_grad, mixer_grad, up_grad_gate, up_grad_lift, down_grad = map(
        added,
        exchange(
            ids,
            swap(COL, contract_cols(gathered_dproj, proj_matrix)),
            (DP, proj_part, False),
            swap(DP, contract_rows(gathered_gated, gathered_dres)),
            swap(DP, contract_rows(gathered_dgate, gathered_two)),
            swap(DP, contract_rows(gathered_dlift, gathered_two)),
            swap(DP, down_part),
        ),
    )
    gains_part = jnp.stack(
        [
            gain_sums(block_input, inverse_one, d_normed_one),
            gain_sums(residual_two, inverse_two, d_normed_two),
        ]
    )
    stats, gains_parts = exchange(
        ids,
        gather(ROW, back_sums(block_input, gain_one, d_normed_one)),
        gather(("dp", "col"), gains_part),
    )
    input_grad = d_residual + norm_back(
        block_input, inverse_one, gain_one, d_normed_one, added(stats)[0]
    )
    proj_grad = proj_grad.transpose(1, 0, 2)
    up_grad = jnp.stack([up_grad_gate, up_grad_lift]).transpose(2, 0, 1)
    conv_grad = lax.dynamic_slice_in_dim(
        added(conv_parts), lax.axis_index("dp") * shard_width, shard_width, 1
    )
    gains_grad = added(gains_parts)
    proj_new, proj_moments_new = adam_step(
        proj_weight, proj_grad, proj_moments, matrix_rate, decay_rate
    )
    conv_new, conv_moments_new = adam_step(conv_weight, conv_grad, conv_moments, small_rate, 0.0)
    mixer_new, mixer_moments_new = adam_step(
        mixer_weight, mixer_grad, mixer_moments, matrix_rate, decay_rate
    )
    up_new, up_moments_new = adam_step(up_weight, up_grad, up_moments, matrix_rate, decay_rate)
    down_new, down_moments_new = adam_step(
        down_weight, down_grad, down_moments, matrix_rate, decay_rate
    )
    gains_new, gains_moments_new = adam_step(norm_gains, gains_grad, gains_moments, small_rate, 0.0)
    return (
        block_output,
        input_grad,
        proj_grad,
        conv_grad,
        mixer_grad,
        up_grad,
        down_grad,
        gains_grad,
        proj_new,
        conv_new,
        mixer_new,
        up_new,
        down_new,
        gains_new,
        proj_moments_new,
        conv_moments_new,
        mixer_moments_new,
        up_moments_new,
        down_moments_new,
        gains_moments_new,
    )


def solution(mesh):
    in_specs = (
        P(("dp", "col"), "row"),
        P(("dp", "col"), "row"),
        P("row", None, ("dp", "col")),
        P(None, ("dp", "col")),
        P(("dp", "col"), "row"),
        P("row", None, ("dp", "col")),
        P(("dp", "col"), "row"),
        P(None, "row"),
        P(None, "row", None, ("dp", "col")),
        P(None, None, ("dp", "col")),
        P(None, ("dp", "col"), "row"),
        P(None, "row", None, ("dp", "col")),
        P(None, ("dp", "col"), "row"),
        P(None, None, "row"),
    )
    out_specs = (
        P(("dp", "col"), "row"),
        P(("dp", "col"), "row"),
        P("row", None, ("dp", "col")),
        P(None, ("dp", "col")),
        P(("dp", "col"), "row"),
        P("row", None, ("dp", "col")),
        P(("dp", "col"), "row"),
        P(None, "row"),
        P("row", None, ("dp", "col")),
        P(None, ("dp", "col")),
        P(("dp", "col"), "row"),
        P("row", None, ("dp", "col")),
        P(("dp", "col"), "row"),
        P(None, "row"),
        P(None, "row", None, ("dp", "col")),
        P(None, None, ("dp", "col")),
        P(None, ("dp", "col"), "row"),
        P(None, "row", None, ("dp", "col")),
        P(None, ("dp", "col"), "row"),
        P(None, None, "row"),
    )
    return jax.shard_map(
        on_device, mesh=mesh, in_specs=in_specs, out_specs=out_specs, check_vma=False
    )
```
